32 devices in a mesh: seq: 8 (over z, y), head: 4 (over x, core).
Axes of the slice: x: 2, y: 2, z: 4, core: 2. Of those that a mesh axis runs over, the one named last changes fastest.
Arguments:
- queries: bfloat16 [4096, 16, 128], P(('seq', 'head')), may hold values from -6 to 6
- keys: bfloat16 [4096, 16, 128], P(('seq', 'head')), may hold values from -6 to 6
- values: bfloat16 [4096, 16, 128], P(('seq', 'head')), may hold values from -6 to 6
- out_grad: bfloat16 [4096, 16, 128], P(('seq', 'head')), may hold values from -6 to 6
- segment_ids: int32 [4096], P('seq'), may hold values from 0 to 3, never falling along the last dimension, each value on 1 to 2048 neighbouring positions
Outputs:
- attended: bfloat16 [4096, 16, 128], P(('seq', 'head'))
- grad_queries: bfloat16 [4096, 16, 128], P(('seq', 'head'))
- grad_keys: bfloat16 [4096, 16, 128], P(('seq', 'head'))
- grad_values: bfloat16 [4096, 16, 128], P(('seq', 'head'))
The draws below stay inside these ranges and needn't reach their ends.
Inputs may be any that keep to these rules, and one draw needn't show every extreme that they name: `segment_ids`: segment numbers never fall along the sequence; each number covers 1 to 2048 consecutive positions, and one covers exactly 2048.
All inputs are finite; a program needn't handle non-finite values.
Results may differ from the reference program's by a relative error of at most 0.03.
Values may be sent and summed in bfloat16 or wider, within the bound.
A program may use at most 64 MiB of HBM per device.

```python
import math
import jax
import jax.numpy as jnp
import numpy as np
from jax import lax

HEADS = 16
HEAD_DIM = 128
BLOCK = 512
TOKENS = 4096
SEGMENTS = 4
SEG_MOST = 2048
N_SEQ = 8


def shard_levels(own_key, dims, shards, smallest, high):
    def one(axis_at, parts):
        heights = jax.random.uniform(jax.random.fold_in(jax.random.fold_in(own_key, 6), axis_at), (parts,), jnp.float32, smallest / len(shards), high / len(shards))
        return jnp.repeat(jnp.exp(heights), dims[axis_at] // parts).reshape((-1,) + (1,) * (len(dims) - axis_at - 1))

    gain = one(*shards[0])
    for cut in shards[1:]:
        gain = gain * one(*cut)
    return gain


def length_profile(amount, total, bound, slope):
    portions = [(1 << 20) // math.isqrt(grade ** slope) + 1 for grade in range(2, amount + 1)]
    surplus, holding = total - bound - (amount - 1), [1] * (amount - 1)
    while surplus > 0:
        free = [i for i in range(amount - 1) if holding[i] < bound]
        mass, left = sum([portions[i] for i in free]), surplus
        for i in free:
            addition = min(bound - holding[i], max(1, left * portions[i] // mass), surplus)
            holding[i] = holding[i] + addition
            surplus = surplus - addition
    return np.array([bound] + holding)


def ragged_sizes(stream_key, count, total, bound, lean):
    if count == 2:
        one = jax.random.randint(stream_key, (), max(1, total - bound), min(bound, total - 1) + 1)
        return jnp.stack([one, total - one])
    lengths = jnp.asarray(length_profile(count, total, bound, lean), jnp.int32)
    twos = (count - 1) // 2
    donor, taker = lengths[1:1 + 2 * twos:2], lengths[2:2 + 2 * twos:2]
    room = jnp.minimum(donor - 1, bound - taker)
    moved = jax.random.randint(jax.random.fold_in(stream_key, 1), (twos,), 0, 1 << 20) % (room + 1)
    lengths = lengths.at[1:1 + 2 * twos:2].set(donor - moved).at[2:2 + 2 * twos:2].set(taker + moved)
    return lengths[jax.random.permutation(jax.random.fold_in(stream_key, 2), count)]


def centred(rng, extent, scale, limit, split=(), kind=jnp.bfloat16):
    values = jax.random.normal(rng, extent, jnp.float32) * scale
    if len(split) > 0:
        values = shard_levels(rng, extent, split, -0.22, 0.18) * values
    return jnp.clip(values, min=-limit, max=limit).astype(kind)


def setup_inputs(seed: int = 0) -> dict:
    seeds = jax.random.split(jax.random.key(seed), 6)
    return {
        "queries": centred(seeds[0], (TOKENS, HEADS, HEAD_DIM), 1.0, 6.0, ((0, 32),)),
        "keys": centred(seeds[1], (TOKENS, HEADS, HEAD_DIM), 1.0, 6.0, ((0, 32),)),
        "values": centred(seeds[2], (TOKENS, HEADS, HEAD_DIM), 1.0, 6.0, ((0, 32),)),
        "out_grad": centred(seeds[3], (TOKENS, HEADS, HEAD_DIM), 1.0, 6.0, ((0, 32),)),
        "segment_ids": jnp.searchsorted(jnp.cumsum(ragged_sizes(seeds[4], SEGMENTS, TOKENS, SEG_MOST, 2)), jnp.arange(TOKENS), side="right").astype(jnp.int32),
    }


HIGH = lax.Precision.HIGHEST

def features(x):
    return jax.nn.elu(x) + 1.0

def rounded(x):
    return lax.optimization_barrier(x.astype(jnp.bfloat16)).astype(jnp.float32)

def attend_local(q32, k32, v32, seg, state, norm, mask_in):
    fq = features(q32)
    fk = features(k32)
    scores = jnp.einsum('thd,shd->hts', rounded(fq), rounded(fk), precision=HIGH)
    count = seg.shape[0]
    place = lax.iota(jnp.int32, count)
    keep = (place[:, None] >= place[None, :]) & (seg[:, None] == seg[None, :])
    scores = jnp.where(keep[None], scores, 0.0)
    numer = jnp.einsum('hts,shd->thd', rounded(scores), rounded(v32), precision=HIGH)
    fq_in = fq * mask_in[:, None, None]
    numer = numer + jnp.einsum('thd,hde->the', fq_in, state, precision=HIGH)
    denom = lax.optimization_barrier(jnp.sum(scores, axis=2)).T + jnp.einsum('thd,hd->th', fq_in, norm, precision=HIGH)
    return numer / denom[:, :, None]

def summarize(k32, v32, seg):
    closing = (seg == seg[-1]).astype(jnp.float32)
    fk = features(k32) * closing[:, None, None]
    state = jnp.einsum('thd,the->hde', rounded(fk), rounded(v32), precision=HIGH)
    return (state, lax.optimization_barrier(jnp.sum(fk, axis=0)))

def reference(queries, keys, values, out_grad, segment_ids):

    def forward(q32, k32, v32):

        def step(carry, block):
            state, norm, previous = carry
            qb, kb, vb, seg = block
            mask_in = (seg == previous).astype(jnp.float32)
            quotient = attend_local(qb, kb, vb, seg, state, norm, mask_in)
            add_state, add_norm = summarize(kb, vb, seg)
            whole = seg[-1] == previous
            new_state = jnp.where(whole, state, 0.0) + add_state
            new_norm = jnp.where(whole, norm, 0.0) + add_norm
            return ((new_state, new_norm, seg[-1]), quotient)
        shaped = (q32.reshape(N_SEQ, BLOCK, HEADS, HEAD_DIM), k32.reshape(N_SEQ, BLOCK, HEADS, HEAD_DIM), v32.reshape(N_SEQ, BLOCK, HEADS, HEAD_DIM), segment_ids.reshape(N_SEQ, BLOCK))
        start = (jnp.zeros((HEADS, HEAD_DIM, HEAD_DIM), jnp.float32), jnp.zeros((HEADS, HEAD_DIM), jnp.float32), jnp.int32(-1))
        _, quotients = lax.scan(jax.checkpoint(step), start, shaped)
        return quotients.reshape(TOKENS, HEADS, HEAD_DIM)
    quotient, pull = jax.vjp(forward, queries.astype(jnp.float32), keys.astype(jnp.float32), values.astype(jnp.float32))
    grad_q, grad_k, grad_v = pull(out_grad.astype(jnp.float32))
    return (quotient.astype(jnp.bfloat16), grad_q.astype(jnp.bfloat16), grad_k.astype(jnp.bfloat16), grad_v.astype(jnp.bfloat16))
```

```python
import functools

import jax
import jax.numpy as jnp
from jax import lax
from jax.experimental import pallas as pl
from jax.experimental.pallas import tpu as pltpu
from jax.sharding import PartitionSpec as P

F32 = jnp.float32
BF16 = jnp.bfloat16
MESH = pl.DeviceIdType.MESH


def features(x):
    return jnp.where(x > 0, x + 1.0, jnp.exp(jnp.minimum(x, 0.0)))


def mm(a, b, ca, cb):
    return lax.dot_general(a, b, (((ca,), (cb,)), ((), ())), preferred_element_type=F32)


def kernel(seqs, group, window, coef, col, row, q_ref, k_ref, v_ref, g_ref,
           o_ref, dq_ref, dk_ref, dv_ref,
           fq_s, fk_s, sb_s, dn_s, inv_s, num_s, p2_s, gk_s,
           nst, n1, n2st, n2, nin,
           mst, m1, m2st, m2, cnm,
           sst, s1, s2st, s2, s3st, sin,
           gst, g1, g2st, g2, g3st, cin,
           acc,
           send1, recv1, send2, recv2):
    r = lax.axis_index("seq")
    h = lax.axis_index("head")
    heads, rows, dim = q_ref.shape
    own = heads // group
    mine = pl.ds(h * own, own)

    barrier = pltpu.get_barrier_semaphore()
    for i in range(1, group):
        pl.semaphore_signal(barrier, inc=1, device_id=(r, lax.rem(h + i, group)), device_id_type=MESH)
    for d in range(1, window + 1):
        @pl.when(r + d < seqs)
        def _():
            pl.semaphore_signal(barrier, inc=1, device_id=(r + d, h), device_id_type=MESH)

        @pl.when(r >= d)
        def _():
            pl.semaphore_signal(barrier, inc=1, device_id=(r - d, h), device_id_type=MESH)

    o_ft = 0
    o_bt = o_ft + group
    o_cf = o_bt + group
    o_cb = o_cf + group * group
    o_mf = o_cb + group * group
    o_mb = o_mf + group
    o_sc = o_mb + group
    first_block, last_block = coef[o_sc], coef[o_sc + 1]
    opens, closes = coef[o_sc + 2], coef[o_sc + 3]
    enter = col[:, 0:1]
    leave = col[:, 1:2]
    seg_c = col[:, 2:3]
    seg_r = row[0:1, :]
    keep = (lax.broadcasted_iota(jnp.int32, (rows, rows), 0)
            >= lax.broadcasted_iota(jnp.int32, (rows, rows), 1)) & (seg_c == seg_r)

    def inside(kind, i, src, dst):
        return pltpu.make_async_remote_copy(
            src_ref=src, dst_ref=dst, send_sem=send1.at[kind, i], recv_sem=recv1.at[kind, i],
            device_id=(r, lax.rem(h + i, group)), device_id_type=MESH)

    def along(kind, d, sign, src, dst):
        return pltpu.make_async_remote_copy(
            src_ref=src, dst_ref=dst, send_sem=send2.at[kind, d], recv_sem=recv2.at[kind, d],
            device_id=(r + sign * d, h), device_id_type=MESH)

    def has_to(d, sign):
        return (r + d < seqs) if sign > 0 else (r >= d)

    def has_from(d, sign):
        return (r >= d) if sign > 0 else (r + d < seqs)

    def stage1(a, c):
        fk = features(k_ref[a].astype(F32))
        fq = features(q_ref[a].astype(F32))
        fq_s[a] = fq.astype(BF16)
        fkb = fk.astype(BF16)
        fk_s[a] = fkb
        closing = fk * leave
        nst[pl.ds(a, 1), :] = jnp.sum(closing, axis=0, keepdims=True)
        sst[a] = mm(closing.astype(BF16), v_ref[a], 0, 0).astype(BF16)
        return c

    lax.fori_loop(0, heads, stage1, 0)

    peers = group - 1
    for d in range(1, window + 1):
        peers = peers + jnp.where(r >= d, 1, 0) + jnp.where(r + d < seqs, 1, 0)
    pl.semaphore_wait(barrier, peers)

    def small_send(kind, st, buf):
        for i in range(1, group):
            inside(kind, i, st, buf.at[i]).start()

    def big_send(kind, st, buf):
        for i in range(1, group):
            inside(kind, i, st.at[pl.ds(lax.rem(h + i, group) * own, own)], buf.at[h]).start()

    def inside_wait(kind, src, dst):
        for i in range(1, group):
            inside(kind, i, src, dst).wait()

    def small_total(base, st, buf):
        total = coef[base + h] * st[...]
        for i in range(1, group):
            total = total + coef[base + lax.rem(h - i + group, group)] * buf[i]
        return total

    small_send(0, nst, n1)
    big_send(1, sst, s1)

    def stage2(a, c):
        s = jnp.where(keep, mm(fq_s[a], fk_s[a], 1, 1), 0.0)
        inv_s[a] = jnp.sum(s, axis=1, keepdims=True)
        sb_s[a] = s.astype(BF16)
        return c

    lax.fori_loop(0, heads, stage2, 0)

    def small_along(kind, sign, st, buf, value, tag):
        st[pl.ds(0, heads), :] = value
        st[pl.ds(heads, 8), :] = jnp.full((8, dim), tag, F32)
        for d in range(1, window + 1):
            @pl.when(has_to(d, sign))
            def _():
                along(kind, d, sign, st, buf.at[d]).start()

    def small_along_take(kind, sign, st, buf, out, scale, own_tag):
        for d in range(1, window + 1):
            @pl.when(has_from(d, sign))
            def _():
                along(kind, d, sign, st, buf.at[d]).wait_recv()
                linked = buf[d, pl.ds(heads, 1), :] == own_tag
                out[...] += jnp.where(linked, buf[d, pl.ds(0, heads), :], 0.0) * scale

    def along_sent(kind, sign, st, buf):
        for d in range(1, window + 1):
            @pl.when(has_to(d, sign))
            def _():
                along(kind, d, sign, st, buf.at[d]).wait_send()

    def big_along(kind, sign, base, st, mid, out, buf):
        mid[h] = st[mine]
        for a in range(own):
            total = coef[base] * mid[0, a].astype(F32)
            for j in range(1, group):
                total = total + coef[base + j] * mid[j, a].astype(F32)
            out[a] = total.astype(BF16)
        for d in range(1, window + 1):
            @pl.when(has_to(d, sign))
            def _():
                along(kind, d, sign, out, buf.at[d]).start()

    def big_back(kind, sign, kind1, small, tag, base_p, base_c, mid, out, buf, st3, fin):
        acc[...] = jnp.zeros_like(acc)
        for d in range(1, window + 1):
            @pl.when(has_from(d, sign))
            def _():
                along(kind, d, sign, out, buf.at[d]).wait_recv()
                linked = small[d, pl.ds(heads, 1), :] == tag
                for a in range(own):
                    acc[a] += jnp.where(linked, buf[d, a].astype(F32), 0.0)
        for j in range(group):
            others = range(j) if sign > 0 else range(j + 1, group)
            for a in range(own):
                total = coef[base_p + j] * acc[a]
                for m in others:
                    total = total + coef[base_c + j * group + m] * mid[m, a].astype(F32)
                st3[j, a] = total.astype(BF16)
        for i in range(1, group):
            inside(kind1, i, st3.at[lax.rem(h + i, group)], fin.at[mine]).start()
        fin[mine] = st3[h]

    inside_wait(0, nst, n1.at[1])
    small_along(0, 1, n2st, n2, small_total(o_ft, nst, n1), last_block)
    inside_wait(1, sst.at[mine], s1.at[0])
    big_along(1, 1, o_ft, sst, s1, s2st, s2)
    nin[...] = small_total(o_mf, nst, n1)
    small_along_take(0, 1, n2st, n2, nin, opens, first_block)

    def stage4(a, c):
        fq = features(q_ref[a].astype(F32)) * enter
        denom = inv_s[a] + jnp.sum(fq * nin[pl.ds(a, 1), :], axis=1, keepdims=True)
        inv = 1.0 / denom
        inv_s[a] = inv
        dn = (g_ref[a].astype(F32) * inv).astype(BF16)
        dn_s[a] = dn
        gst[a] = mm(fq.astype(BF16), dn, 0, 0).astype(BF16)
        return c

    lax.fori_loop(0, heads, stage4, 0)
    big_send(2, gst, g1)

    def stage5(a, c):
        num_s[a] = mm(sb_s[a], v_ref[a], 1, 0)
        p2_s[a] = mm(dn_s[a], v_ref[a], 1, 1)
        return c

    lax.fori_loop(0, heads, stage5, 0)
    inside_wait(2, gst.at[mine], g1.at[0])
    big_along(3, -1, o_bt, gst, g1, g2st, g2)

    big_back(1, 1, 3, n2, first_block, o_bt, o_cf, s1, s2st, s2, s3st, sin)
    inside_wait(3, s3st.at[0], sin.at[mine])

    def stage7(a, c):
        q = q_ref[a].astype(F32)
        fq = features(q)
        st = sin[a]
        inv = inv_s[a]
        numer = num_s[a] + enter * mm(fq_s[a], st, 1, 0)
        quo = numer * inv
        o_ref[a] = quo.astype(BF16)
        dden = -jnp.sum(g_ref[a].astype(F32) * quo, axis=1, keepdims=True) * inv
        inner = enter * dden
        mst[pl.ds(a, 1), :] = jnp.sum(fq * inner, axis=0, keepdims=True)
        ds = jnp.where(keep, p2_s[a] + dden, 0.0).astype(BF16)
        dfq = mm(ds, fk_s[a], 1, 0) + enter * mm(dn_s[a], st, 1, 1) + inner * nin[pl.ds(a, 1), :]
        dq_ref[a] = (dfq * jnp.where(q > 0, 1.0, fq)).astype(BF16)
        gk_s[a] = mm(ds, fq_s[a], 0, 0)
        return c

    lax.fori_loop(0, heads, stage7, 0)
    small_send(4, mst, m1)
    inside_wait(4, mst, m1.at[1])
    small_along(2, -1, m2st, m2, small_total(o_bt, mst, m1), first_block)
    cnm[...] = small_total(o_mb, mst, m1)
    small_along_take(2, -1, m2st, m2, cnm, closes, last_block)

    big_back(3, -1, 5, m2, last_block, o_ft, o_cb, g1, g2st, g2, g3st, cin)
    inside_wait(5, g3st.at[0], cin.at[mine])

    def stage9(a, c):
        k = k_ref[a].astype(F32)
        st = cin[a]
        dv = mm(sb_s[a], dn_s[a], 0, 0) + leave * mm(fk_s[a], st, 1, 0)
        dv_ref[a] = dv.astype(BF16)
        dfk = gk_s[a] + leave * (mm(v_ref[a], st, 1, 1) + cnm[pl.ds(a, 1), :])
        dk_ref[a] = (dfk * jnp.where(k > 0, 1.0, features(k))).astype(BF16)
        return c

    lax.fori_loop(0, heads, stage9, 0)
    along_sent(0, 1, n2st, n2)
    along_sent(1, 1, s2st, s2)
    along_sent(2, -1, m2st, m2)
    along_sent(3, -1, g2st, g2)


def local(queries, keys, values, out_grad, segment_ids):
    seqs, group = lax.axis_size("seq"), lax.axis_size("head")
    block = segment_ids.shape[0]
    rows, heads, dim = queries.shape
    own = heads // group
    longest = min(12 * block, block * seqs // 2)
    window = min(-(-longest // block), seqs - 1)
    h = lax.axis_index("head")

    firsts = segment_ids[::rows]
    lasts = segment_ids[rows - 1::rows]
    order = lax.iota(jnp.int32, group)
    cf = (lasts[None, :] == firsts[:, None]) & (order[None, :] < order[:, None])
    cb = (firsts[None, :] == lasts[:, None]) & (order[None, :] > order[:, None])
    ft = lasts == segment_ids[-1]
    bt = firsts == segment_ids[0]
    cf, cb, ft, bt = (x.astype(F32) for x in (cf, cb, ft, bt))
    ends = jnp.stack([segment_ids[0], segment_ids[-1]]).astype(F32)
    coef = jnp.concatenate([
        ft, bt, cf.reshape(-1), cb.reshape(-1), cf[h], cb[h], ends,
        jnp.stack([bt[h], ft[h]]),
    ])
    seg = lax.dynamic_slice(segment_ids, (h * rows,), (rows,))
    col = jnp.stack([seg == seg[0], seg == seg[-1]], axis=1).astype(F32)
    segf = seg.astype(F32)
    col = jnp.concatenate([col, segf[:, None]], axis=1)
    row = segf[None, :]

    turned = [x.transpose(1, 0, 2) for x in (queries, keys, values, out_grad)]
    vmem = pl.BlockSpec(memory_space=pltpu.VMEM)
    full = (heads, rows, dim)
    square = (heads, dim, dim)
    small = (heads, dim)
    tagged = (heads + 8, dim)
    piece = (own, dim, dim)
    state_scratch = [
        pltpu.VMEM(square, BF16), pltpu.VMEM((group,) + piece, BF16), pltpu.VMEM(piece, BF16),
        pltpu.VMEM((window + 1,) + piece, BF16), pltpu.VMEM((group,) + piece, BF16), pltpu.VMEM(square, BF16),
    ]
    norm_scratch = [
        pltpu.VMEM(small, F32), pltpu.VMEM((group,) + small, F32), pltpu.VMEM(tagged, F32),
        pltpu.VMEM((window + 1,) + tagged, F32), pltpu.VMEM(small, F32),
    ]
    outs = pl.pallas_call(
        functools.partial(kernel, seqs, group, window),
        out_shape=[jax.ShapeDtypeStruct(full, BF16)] * 4,
        in_specs=[pl.BlockSpec(memory_space=pltpu.SMEM)] + [vmem] * 6,
        out_specs=[vmem] * 4,
        scratch_shapes=[
            pltpu.VMEM(full, BF16), pltpu.VMEM(full, BF16), pltpu.VMEM((heads, rows, rows), BF16),
            pltpu.VMEM(full, BF16), pltpu.VMEM((heads, rows, 1), F32), pltpu.VMEM(full, F32),
            pltpu.VMEM((heads, rows, rows), F32), pltpu.VMEM(full, F32),
        ] + norm_scratch + norm_scratch + state_scratch + state_scratch + [
            pltpu.VMEM(piece, F32),
            pltpu.SemaphoreType.DMA((6, group)), pltpu.SemaphoreType.DMA((6, group)),
            pltpu.SemaphoreType.DMA((4, window + 1)), pltpu.SemaphoreType.DMA((4, window + 1)),
        ],
        compiler_params=pltpu.CompilerParams(
            collective_id=0, has_side_effects=True, vmem_limit_bytes=48 * 1024 * 1024),
        name="segment_attention",
    )(coef, col, row, *turned)
    return tuple(x.transpose(1, 0, 2) for x in outs)


def solution(mesh):
    tokens = P(("seq", "head"), None, None)
    return jax.shard_map(
        local,
        mesh=mesh,
        in_specs=(tokens, tokens, tokens, tokens, P("seq")),
        out_specs=(tokens, tokens, tokens, tokens),
        check_vma=False,
    )
```

```python
import functools

import jax
import jax.numpy as jnp
from jax import lax
from jax.experimental import pallas as pl
from jax.experimental.pallas import tpu as pltpu
from jax.sharding import PartitionSpec as P

F32 = jnp.float32
BF16 = jnp.bfloat16
MESH = pl.DeviceIdType.MESH


def features(x):
    return jnp.where(x > 0, x + 1.0, jnp.exp(jnp.minimum(x, 0.0)))


def mm(a, b, ca, cb):
    return lax.dot_general(a, b, (((ca,), (cb,)), ((), ())), preferred_element_type=F32)


def kernel(seqs, group, window, ids_ref, seg_ref, q_ref, k_ref, v_ref, g_ref,
           o_ref, dq_ref, dk_ref, dv_ref,
           fq_s, fk_s, sb_s, dn_s, inv_s, num_s, p2_s, gk_s,
           nst, n1, n2st, n2, nin,
           mst, m1, m2st, m2, cnm,
           sst, s1, s2st, s2, s3st, sin,
           gst, g1, g2st, g2, g3st, cin,
           tagst, tags,
           send1, recv1, send2, recv2):
    r = lax.axis_index("seq")
    h = lax.axis_index("head")
    heads, rows, dim = q_ref.shape
    own = heads // group

    barrier = pltpu.get_barrier_semaphore()
    for i in range(1, group):
        pl.semaphore_signal(barrier, inc=1, device_id=(r, lax.rem(h + i, group)), device_id_type=MESH)
    for d in range(1, window + 1):
        @pl.when(r + d < seqs)
        def _():
            pl.semaphore_signal(barrier, inc=1, device_id=(r + d, h), device_id_type=MESH)

        @pl.when(r >= d)
        def _():
            pl.semaphore_signal(barrier, inc=1, device_id=(r - d, h), device_id_type=MESH)

    def same(x, y):
        return jnp.where(x == y, 1.0, 0.0)

    ids = [(ids_ref[j * rows], ids_ref[(j + 1) * rows - 1]) for j in range(group)]
    id_first, id_last = ids[0][0], ids[-1][1]
    my_first, my_last = ids_ref[h * rows], ids_ref[h * rows + rows - 1]
    first_block, last_block = id_first.astype(F32), id_last.astype(F32)
    opens, closes = same(my_first, id_first), same(my_last, id_last)
    seg_r = seg_ref[pl.ds(h, 1), :]
    seg_c = jnp.transpose(jnp.broadcast_to(seg_r, (rows, rows)))[:, 0:1]
    enter = jnp.where(seg_c == my_first.astype(F32), 1.0, 0.0)
    leave = jnp.where(seg_c == my_last.astype(F32), 1.0, 0.0)
    keep = (lax.broadcasted_iota(jnp.int32, (rows, rows), 0)
            >= lax.broadcasted_iota(jnp.int32, (rows, rows), 1)) & (seg_c == seg_r)

    def inside(kind, a, i, src, dst):
        return pltpu.make_async_remote_copy(
            src_ref=src, dst_ref=dst, send_sem=send1.at[kind, a, i], recv_sem=recv1.at[kind, a, i],
            device_id=(r, lax.rem(h + i, group)), device_id_type=MESH)

    def along(kind, a, d, sign, src, dst):
        return pltpu.make_async_remote_copy(
            src_ref=src, dst_ref=dst, send_sem=send2.at[kind, a, d], recv_sem=recv2.at[kind, a, d],
            device_id=(r + sign * d, h), device_id_type=MESH)

    def has_to(d, sign):
        return (r + d < seqs) if sign > 0 else (r >= d)

    def has_from(d, sign):
        return (r >= d) if sign > 0 else (r + d < seqs)

    def each_to(sign, act):
        for d in range(1, window + 1):
            pl.when(has_to(d, sign))(functools.partial(act, d))

    def each_from(sign, act):
        for d in range(1, window + 1):
            pl.when(has_from(d, sign))(functools.partial(act, d))

    for d in range(1, window + 1):
        @pl.when(r < d)
        def _():
            n2[d] = jnp.full(n2.shape[1:], -1.0, F32)

        @pl.when(r + d >= seqs)
        def _():
            m2[d] = jnp.full(m2.shape[1:], -1.0, F32)
            tags[d] = jnp.full(tags.shape[1:], -1.0, F32)

    def staged(work, count, step):
        def body(t, c):
            done = [work(t * step + u) for u in range(step)]
            for puts in done:
                for ref, at, value in puts:
                    ref[at] = value
            return c

        lax.fori_loop(0, count // step, body, 0)

    def piece(work, a):
        done = [work(j * own + a) for j in range(group)]
        for puts in done:
            for ref, at, value in puts:
                ref[at] = value

    def row_of(a):
        return (pl.ds(a, 1), slice(None))

    def small_total(weigh, st, buf):
        total = weigh(h) * st[...]
        for i in range(1, group):
            total = total + weigh(lax.rem(h - i + group, group)) * buf[i]
        return total

    def closing(j):
        return same(ids_ref[j * rows + rows - 1], id_last)

    def opening(j):
        return same(ids_ref[j * rows], id_first)

    def earlier(j):
        return jnp.where(j < h, same(ids_ref[j * rows + rows - 1], my_first), 0.0)

    def later(j):
        return jnp.where(j > h, same(ids_ref[j * rows], my_last), 0.0)

    def small_send(kind, st, buf):
        for i in range(1, group):
            inside(kind, 0, i, st, buf.at[i]).start()

    def small_wait(kind, st, buf):
        for i in range(1, group):
            inside(kind, 0, i, st, buf.at[i]).wait()

    def small_along(kind, sign, st, buf, value, tag):
        st[pl.ds(0, heads), :] = value
        st[pl.ds(heads, 8), :] = jnp.full((8, dim), tag, F32)
        each_to(sign, lambda d: along(kind, 0, d, sign, st, buf.at[d]).start())

    def small_along_take(kind, sign, st, buf, scale, own_tag):
        each_from(sign, lambda d: along(kind, 0, d, sign, st, buf.at[d]).wait_recv())
        total = jnp.zeros((heads, dim), F32)
        for d in range(1, window + 1):
            linked = buf[d, pl.ds(heads, 1), :] == own_tag
            total = total + jnp.where(linked, buf[d, pl.ds(0, heads), :], 0.0)
        return total * scale

    def big_send(kind, a, st, buf):
        for i in range(1, group):
            inside(kind, a, i, st.at[lax.rem(h + i, group) * own + a], buf.at[h, a]).start()

    def big_along(kind, kind1, a, sign, weigh, st, mid, out, buf):
        for i in range(1, group):
            inside(kind1, a, i, st.at[a], mid.at[0, a]).wait()
        mid[h, a] = st[h * own + a]
        total = weigh(0) * mid[0, a].astype(F32)
        for j in range(1, group):
            total = total + weigh(j) * mid[j, a].astype(F32)
        out[a] = total.astype(BF16)
        each_to(sign, lambda d: along(kind, a, d, sign, out.at[a], buf.at[d, a]).start())

    def big_back(kind, kind1, a, sign, tag_of, tag, mid, out, buf, st3, fin):
        each_from(sign, lambda d: along(kind, a, d, sign, out.at[a], buf.at[d, a]).wait_recv())
        far = jnp.zeros((dim, dim), F32)
        for d in range(1, window + 1):
            far = far + jnp.where(tag_of(d) == tag, buf[d, a].astype(F32), 0.0)
        near = [mid[m, a].astype(F32) for m in range(group)]
        for j in range(group):
            if sign > 0:
                total = same(ids[j][0], id_first) * far
                for m in range(j):
                    total = total + same(ids[m][1], ids[j][0]) * near[m]
            else:
                total = same(ids[j][1], id_last) * far
                for m in range(j + 1, group):
                    total = total + same(ids[m][0], ids[j][1]) * near[m]
            st3[j, a] = total.astype(BF16)
        for i in range(1, group):
            inside(kind1, a, i, st3.at[lax.rem(h + i, group), a], fin.at[h * own + a]).start()
        fin[h * own + a] = st3[h, a]

    def back_wait(kind1, a, st3, fin):
        for i in range(1, group):
            inside(kind1, a, i, st3.at[0, a], fin.at[a]).wait()

    def over(body):
        def turn(a, c):
            body(a)
            return c

        lax.fori_loop(0, own, turn, 0)

    def features_of(a):
        fk = features(k_ref[a].astype(F32))
        fq = features(q_ref[a].astype(F32))
        return [(fq_s, a, fq.astype(BF16)), (fk_s, a, fk.astype(BF16)),
                (nst, row_of(a), jnp.sum(fk * leave, axis=0, keepdims=True))]

    def state_of(a):
        ending = (fk_s[a].astype(F32) * leave).astype(BF16)
        return [(sst, a, mm(ending, v_ref[a], 0, 0).astype(BF16))]

    staged(features_of, heads, 4)

    peers = group - 1
    for d in range(1, window + 1):
        peers = peers + jnp.where(r >= d, 1, 0) + jnp.where(r + d < seqs, 1, 0)
    pl.semaphore_wait(barrier, peers)

    small_send(0, nst, n1)
    tagst[...] = jnp.full(tagst.shape, first_block, F32)
    each_to(-1, lambda d: along(4, 0, d, -1, tagst, tags.at[d]).start())

    def open_states(a):
        piece(state_of, a)
        big_send(1, a, sst, s1)

    over(open_states)

    def scores_of(a):
        s = jnp.where(keep, mm(fq_s[a], fk_s[a], 1, 1), 0.0)
        return [(inv_s, a, jnp.sum(s, axis=1, keepdims=True)), (sb_s, a, s.astype(BF16))]

    small_wait(0, nst, n1)
    small_along(0, 1, n2st, n2, small_total(closing, nst, n1), last_block)
    staged(scores_of, heads, 4)
    nin[...] = small_total(earlier, nst, n1) + small_along_take(0, 1, n2st, n2, opens, first_block)

    def gradient_state_of(a):
        fq = features(q_ref[a].astype(F32)) * enter
        denom = inv_s[a] + jnp.sum(fq * nin[pl.ds(a, 1), :], axis=1, keepdims=True)
        inv = 1.0 / denom
        dn = (g_ref[a].astype(F32) * inv).astype(BF16)
        return [(inv_s, a, inv), (dn_s, a, dn), (gst, a, mm(fq.astype(BF16), dn, 0, 0).astype(BF16))]

    def gradient_states(a):
        piece(gradient_state_of, a)
        big_send(2, a, gst, g1)
        big_along(1, 1, a, 1, closing, sst, s1, s2st, s2)

    over(gradient_states)

    def inner_of(a):
        return [(num_s, a, mm(sb_s[a], v_ref[a], 1, 0)), (p2_s, a, mm(dn_s[a], v_ref[a], 1, 1))]

    staged(inner_of, heads, 4)
    over(lambda a: big_along(3, 2, a, -1, opening, gst, g1, g2st, g2))

    over(lambda a: big_back(1, 3, a, 1, lambda d: n2[d, pl.ds(heads, 1), :], first_block, s1, s2st, s2, s3st, sin))
    each_from(-1, lambda d: along(4, 0, d, -1, tagst, tags.at[d]).wait_recv())

    def quotient_of(a):
        q = q_ref[a].astype(F32)
        fq = features(q)
        st = sin[a]
        inv = inv_s[a]
        numer = num_s[a] + enter * mm(fq_s[a], st, 1, 0)
        quo = numer * inv
        dden = -jnp.sum(g_ref[a].astype(F32) * quo, axis=1, keepdims=True) * inv
        inner = enter * dden
        ds = jnp.where(keep, p2_s[a] + dden, 0.0).astype(BF16)
        dfq = mm(ds, fk_s[a], 1, 0) + enter * mm(dn_s[a], st, 1, 1) + inner * nin[pl.ds(a, 1), :]
        return [(o_ref, a, quo.astype(BF16)),
                (mst, row_of(a), jnp.sum(fq * inner, axis=0, keepdims=True)),
                (dq_ref, a, (dfq * jnp.where(q > 0, 1.0, fq)).astype(BF16)),
                (gk_s, a, mm(ds, fq_s[a], 0, 0))]

    def quotients(a):
        back_wait(3, a, s3st, sin)
        piece(quotient_of, a)
        big_back(3, 5, a, -1, lambda d: tags[d, pl.ds(0, 1), :], last_block, g1, g2st, g2, g3st, cin)

    over(quotients)
    small_send(4, mst, m1)

    def values_of(a):
        dv = mm(sb_s[a], dn_s[a], 0, 0) + leave * mm(fk_s[a], cin[a], 1, 0)
        return [(dv_ref, a, dv.astype(BF16))]

    def keys_of(a):
        return [(gk_s, a, gk_s[a] + leave * mm(v_ref[a], cin[a], 1, 1))]

    def finish_of(a):
        k = k_ref[a].astype(F32)
        dfk = gk_s[a] + leave * cnm[pl.ds(a, 1), :]
        return [(dk_ref, a, (dfk * jnp.where(k > 0, 1.0, features(k))).astype(BF16))]

    small_wait(4, mst, m1)
    small_along(2, -1, m2st, m2, small_total(opening, mst, m1), first_block)

    def values(a):
        back_wait(5, a, g3st, cin)
        piece(values_of, a)
        piece(keys_of, a)

    over(values)
    cnm[...] = small_total(later, mst, m1) + small_along_take(2, -1, m2st, m2, closes, last_block)
    staged(finish_of, heads, 4)

    each_to(1, lambda d: along(0, 0, d, 1, n2st, n2.at[d]).wait_send())
    each_to(-1, lambda d: along(2, 0, d, -1, m2st, m2.at[d]).wait_send())
    each_to(-1, lambda d: along(4, 0, d, -1, tagst, tags.at[d]).wait_send())

    def sent(a):
        each_to(1, lambda d: along(1, a, d, 1, s2st.at[a], s2.at[d, a]).wait_send())
        each_to(-1, lambda d: along(3, a, d, -1, g2st.at[a], g2.at[d, a]).wait_send())

    over(sent)


def local(queries, keys, values, out_grad, segment_ids):
    seqs, group = lax.axis_size("seq"), lax.axis_size("head")
    block = segment_ids.shape[0]
    rows, heads, dim = queries.shape
    own = heads // group
    longest = min(12 * block, block * seqs // 2)
    window = min(-(-longest // block), seqs - 1)
    turned = [x.transpose(1, 0, 2) for x in (queries, keys, values, out_grad)]
    vmem = pl.BlockSpec(memory_space=pltpu.VMEM)
    full = (heads, rows, dim)
    square = (heads, dim, dim)
    small = (heads, dim)
    tagged = (heads + 8, dim)
    piece = (own, dim, dim)
    state_scratch = [
        pltpu.VMEM(square, BF16), pltpu.VMEM((group,) + piece, BF16), pltpu.VMEM(piece, BF16),
        pltpu.VMEM((window + 1,) + piece, BF16), pltpu.VMEM((group,) + piece, BF16), pltpu.VMEM(square, BF16),
    ]
    norm_scratch = [
        pltpu.VMEM(small, F32), pltpu.VMEM((group,) + small, F32), pltpu.VMEM(tagged, F32),
        pltpu.VMEM((window + 1,) + tagged, F32), pltpu.VMEM(small, F32),
    ]
    outs = pl.pallas_call(
        functools.partial(kernel, seqs, group, window),
        out_shape=[jax.ShapeDtypeStruct(full, BF16)] * 4,
        in_specs=[pl.BlockSpec(memory_space=pltpu.SMEM)] + [vmem] * 5,
        out_specs=[vmem] * 4,
        scratch_shapes=[
            pltpu.VMEM(full, BF16), pltpu.VMEM(full, BF16), pltpu.VMEM((heads, rows, rows), BF16),
            pltpu.VMEM(full, BF16), pltpu.VMEM((heads, rows, 1), F32), pltpu.VMEM(full, F32),
            pltpu.VMEM((heads, rows, rows), F32), pltpu.VMEM(full, F32),
        ] + norm_scratch + norm_scratch + state_scratch + state_scratch + [
            pltpu.VMEM((8, dim), F32), pltpu.VMEM((window + 1, 8, dim), F32),
            pltpu.SemaphoreType.DMA((6, own, group)), pltpu.SemaphoreType.DMA((6, own, group)),
            pltpu.SemaphoreType.DMA((5, own, window + 1)), pltpu.SemaphoreType.DMA((5, own, window + 1)),
        ],
        compiler_params=pltpu.CompilerParams(
            collective_id=0, has_side_effects=True, vmem_limit_bytes=48 * 1024 * 1024),
        name="segment_attention",
    )(segment_ids, segment_ids.reshape(group, rows).astype(F32), *turned)
    return tuple(x.transpose(1, 0, 2) for x in outs)


def solution(mesh):
    tokens = P(("seq", "head"), None, None)
    return jax.shard_map(
        local,
        mesh=mesh,
        in_specs=(tokens, tokens, tokens, tokens, P("seq")),
        out_specs=(tokens, tokens, tokens, tokens),
        check_vma=False,
    )
```

```python
import functools

import jax
import jax.numpy as jnp
from jax import lax
from jax.experimental import pallas as pl
from jax.experimental.pallas import tpu as pltpu
from jax.sharding import PartitionSpec as P

F32 = jnp.float32
BF16 = jnp.bfloat16
MESH = pl.DeviceIdType.MESH
PAIR = 2


def features(x):
    return jnp.where(x > 0, x + 1.0, jnp.exp(jnp.minimum(x, 0.0)))


def mm(a, b, ca, cb):
    return lax.dot_general(a, b, (((ca,), (cb,)), ((), ())), preferred_element_type=F32)


def kernel(seqs, pair, width, window, ids_ref, seg_ref, q_ref, k_ref, v_ref, g_ref,
           o_ref, dq_ref, dk_ref, dv_ref,
           fq_s, fk_s, sb_s, dn_s, inv_s, num_s, p2_s, gk_s,
           nst, n1, n2st, n2, nin,
           mst, m1, m2st, m2, cnm,
           sst, s1, s2st, s2, s3st, sin,
           gst, g1, g2st, g2, g3st, cin,
           tagst, tags,
           send1, recv1, send2, recv2):
    at_seq = lax.axis_index("seq")
    at_head = lax.axis_index("head")
    heads, rows, dim = q_ref.shape
    group = pair * width
    own = heads // group
    r = lax.div(at_seq, pair)
    h = lax.rem(at_seq, pair) * width + at_head

    def member(i):
        m = lax.rem(h + i, group)
        return (r * pair + lax.div(m, width), lax.rem(m, width))

    barrier = pltpu.get_barrier_semaphore()
    for i in range(1, group):
        pl.semaphore_signal(barrier, inc=1, device_id=member(i), device_id_type=MESH)
    for d in range(1, window + 1):
        @pl.when(r + d < seqs)
        def _():
            pl.semaphore_signal(barrier, inc=1, device_id=(at_seq + d * pair, at_head), device_id_type=MESH)

        @pl.when(r >= d)
        def _():
            pl.semaphore_signal(barrier, inc=1, device_id=(at_seq - d * pair, at_head), device_id_type=MESH)

    def same(x, y):
        return jnp.where(x == y, 1.0, 0.0)

    my_first = ids_ref[at_head * rows].astype(F32)
    my_last = ids_ref[at_head * rows + rows - 1].astype(F32)
    seg_r = seg_ref[pl.ds(at_head, 1), :]
    seg_c = jnp.transpose(jnp.broadcast_to(seg_r, (rows, rows)))[:, 0:1]
    enter = jnp.where(seg_c == my_first, 1.0, 0.0)
    leave = jnp.where(seg_c == my_last, 1.0, 0.0)
    keep = (lax.broadcasted_iota(jnp.int32, (rows, rows), 0)
            >= lax.broadcasted_iota(jnp.int32, (rows, rows), 1)) & (seg_c == seg_r)

    def inside(kind, a, i, src, dst):
        return pltpu.make_async_remote_copy(
            src_ref=src, dst_ref=dst, send_sem=send1.at[kind, a, i], recv_sem=recv1.at[kind, a, i],
            device_id=member(i), device_id_type=MESH)

    def along(kind, a, d, sign, src, dst):
        return pltpu.make_async_remote_copy(
            src_ref=src, dst_ref=dst, send_sem=send2.at[kind, a, d], recv_sem=recv2.at[kind, a, d],
            device_id=(at_seq + sign * d * pair, at_head), device_id_type=MESH)

    def has_to(d, sign):
        return (r + d < seqs) if sign > 0 else (r >= d)

    def has_from(d, sign):
        return (r >= d) if sign > 0 else (r + d < seqs)

    def each_to(sign, act):
        for d in range(1, window + 1):
            pl.when(has_to(d, sign))(functools.partial(act, d))

    def each_from(sign, act):
        for d in range(1, window + 1):
            pl.when(has_from(d, sign))(functools.partial(act, d))

    for d in range(1, window + 1):
        @pl.when(r < d)
        def _():
            n2[d] = jnp.full(n2.shape[1:], -1.0, F32)

        @pl.when(r + d >= seqs)
        def _():
            m2[d] = jnp.full(m2.shape[1:], -1.0, F32)
            tags[d] = jnp.full(tags.shape[1:], -1.0, F32)

    def staged(work, count, step):
        def body(t, c):
            done = [work(t * step + u) for u in range(step)]
            for puts in done:
                for ref, at, value in puts:
                    ref[at] = value
            return c

        lax.fori_loop(0, count // step, body, 0)

    def piece(work, a):
        for low in range(0, group, 4):
            done = [work(j * own + a) for j in range(low, min(low + 4, group))]
            for puts in done:
                for ref, at, value in puts:
                    ref[at] = value

    def row_of(a):
        return (pl.ds(a, 1), slice(None))

    def first_of(j):
        return n1[j, pl.ds(heads, 1), :]

    def last_of(j):
        return n1[j, pl.ds(heads + 1, 1), :]

    def small_total(weigh, buf):
        total = weigh(0) * buf[0, pl.ds(0, heads), :]
        for j in range(1, group):
            total = total + weigh(j) * buf[j, pl.ds(0, heads), :]
        return total

    def closing(j):
        return same(last_of(j), last_of(group - 1))

    def opening(j):
        return same(first_of(j), first_of(0))

    def earlier(j):
        return jnp.where(j < h, 1.0, 0.0) * same(last_of(j), my_first)

    def later(j):
        return jnp.where(j > h, 1.0, 0.0) * same(first_of(j), my_last)

    def small_send(kind, st, buf):
        for i in range(1, group):
            inside(kind, 0, i, st, buf.at[h]).start()
        buf[h] = st[...]

    def small_wait(kind, st, buf):
        for i in range(1, group):
            inside(kind, 0, i, st, buf.at[0]).wait()

    def small_along(kind, sign, st, buf, value, tag):
        st[pl.ds(0, heads), :] = value
        st[pl.ds(heads, 8), :] = jnp.broadcast_to(tag, (8, dim))
        each_to(sign, lambda d: along(kind, 0, d, sign, st, buf.at[d]).start())

    def small_along_take(kind, sign, st, buf, scale, own_tag):
        each_from(sign, lambda d: along(kind, 0, d, sign, st, buf.at[d]).wait_recv())
        total = jnp.zeros((heads, dim), F32)
        for d in range(1, window + 1):
            linked = buf[d, pl.ds(heads, 1), :] == own_tag
            total = total + jnp.where(linked, buf[d, pl.ds(0, heads), :], 0.0)
        return total * scale

    def big_send(kind, a, st, buf):
        for i in range(1, group):
            inside(kind, a, i, st.at[lax.rem(h + i, group) * own + a], buf.at[h, a]).start()

    def big_along(kind, kind1, a, sign, weigh, st, mid, out, buf):
        for i in range(1, group):
            inside(kind1, a, i, st.at[a], mid.at[0, a]).wait()
        mid[h, a] = st[h * own + a]
        total = weigh(0) * mid[0, a].astype(F32)
        for j in range(1, group):
            total = total + weigh(j) * mid[j, a].astype(F32)
        out[a] = total.astype(BF16)
        each_to(sign, lambda d: along(kind, a, d, sign, out.at[a], buf.at[d, a]).start())

    def big_back(kind, kind1, a, sign, tag_of, tag, mid, out, buf, st3, fin):
        each_from(sign, lambda d: along(kind, a, d, sign, out.at[a], buf.at[d, a]).wait_recv())
        far = jnp.zeros((dim, dim), F32)
        for d in range(1, window + 1):
            far = far + jnp.where(tag_of(d) == tag, buf[d, a].astype(F32), 0.0)
        near = [mid[m, a].astype(F32) for m in range(group)]
        for j in range(group):
            if sign > 0:
                total = opening(j) * far
                for m in range(j):
                    total = total + same(last_of(m), first_of(j)) * near[m]
            else:
                total = closing(j) * far
                for m in range(j + 1, group):
                    total = total + same(first_of(m), last_of(j)) * near[m]
            st3[j, a] = total.astype(BF16)
        for i in range(1, group):
            inside(kind1, a, i, st3.at[lax.rem(h + i, group), a], fin.at[h * own + a]).start()
        fin[h * own + a] = st3[h, a]

    def back_wait(kind1, a, st3, fin):
        for i in range(1, group):
            inside(kind1, a, i, st3.at[0, a], fin.at[a]).wait()

    def over(body):
        def turn(a, c):
            body(a)
            return c

        lax.fori_loop(0, own, turn, 0)

    def features_of(a):
        fk = features(k_ref[a].astype(F32))
        fq = features(q_ref[a].astype(F32))
        return [(fq_s, a, fq.astype(BF16)), (fk_s, a, fk.astype(BF16)),
                (nst, row_of(a), jnp.sum(fk * leave, axis=0, keepdims=True))]

    def state_of(a):
        ending = (fk_s[a].astype(F32) * leave).astype(BF16)
        return [(sst, a, mm(ending, v_ref[a], 0, 0).astype(BF16))]

    staged(features_of, heads, 4)

    peers = group - 1
    for d in range(1, window + 1):
        peers = peers + jnp.where(r >= d, 1, 0) + jnp.where(r + d < seqs, 1, 0)
    pl.semaphore_wait(barrier, peers)

    nst[pl.ds(heads, 1), :] = jnp.full((1, dim), my_first, F32)
    nst[pl.ds(heads + 1, 1), :] = jnp.full((1, dim), my_last, F32)
    small_send(0, nst, n1)

    def open_states(a):
        piece(state_of, a)
        big_send(1, a, sst, s1)

    over(open_states)

    def scores_of(a):
        s = jnp.where(keep, mm(fq_s[a], fk_s[a], 1, 1), 0.0)
        return [(inv_s, a, jnp.sum(s, axis=1, keepdims=True)), (sb_s, a, s.astype(BF16))]

    small_wait(0, nst, n1)
    small_along(0, 1, n2st, n2, small_total(closing, n1), last_of(group - 1))
    tagst[...] = jnp.broadcast_to(first_of(0), tagst.shape)
    each_to(-1, lambda d: along(4, 0, d, -1, tagst, tags.at[d]).start())
    staged(scores_of, heads, 4)
    nin[...] = small_total(earlier, n1) + small_along_take(0, 1, n2st, n2, same(first_of(0), my_first), first_of(0))

    def gradient_state_of(a):
        fq = features(q_ref[a].astype(F32)) * enter
        denom = inv_s[a] + jnp.sum(fq * nin[pl.ds(a, 1), :], axis=1, keepdims=True)
        inv = 1.0 / denom
        dn = (g_ref[a].astype(F32) * inv).astype(BF16)
        return [(inv_s, a, inv), (dn_s, a, dn), (gst, a, mm(fq.astype(BF16), dn, 0, 0).astype(BF16))]

    def gradient_states(a):
        piece(gradient_state_of, a)
        big_send(2, a, gst, g1)
        big_along(1, 1, a, 1, closing, sst, s1, s2st, s2)

    over(gradient_states)

    def inner_of(a):
        return [(num_s, a, mm(sb_s[a], v_ref[a], 1, 0)), (p2_s, a, mm(dn_s[a], v_ref[a], 1, 1))]

    staged(inner_of, heads, 4)
    over(lambda a: big_along(3, 2, a, -1, opening, gst, g1, g2st, g2))

    over(lambda a: big_back(1, 3, a, 1, lambda d: n2[d, pl.ds(heads, 1), :], first_of(0), s1, s2st, s2, s3st, sin))
    each_from(-1, lambda d: along(4, 0, d, -1, tagst, tags.at[d]).wait_recv())

    def quotient_of(a):
        q = q_ref[a].astype(F32)
        fq = features(q)
        st = sin[a]
        inv = inv_s[a]
        numer = num_s[a] + enter * mm(fq_s[a], st, 1, 0)
        quo = numer * inv
        dden = -jnp.sum(g_ref[a].astype(F32) * quo, axis=1, keepdims=True) * inv
        inner = enter * dden
        ds = jnp.where(keep, p2_s[a] + dden, 0.0).astype(BF16)
        dfq = mm(ds, fk_s[a], 1, 0) + enter * mm(dn_s[a], st, 1, 1) + inner * nin[pl.ds(a, 1), :]
        return [(o_ref, a, quo.astype(BF16)),
                (mst, row_of(a), jnp.sum(fq * inner, axis=0, keepdims=True)),
                (dq_ref, a, (dfq * jnp.where(q > 0, 1.0, fq)).astype(BF16)),
                (gk_s, a, mm(ds, fq_s[a], 0, 0))]

    def quotients(a):
        back_wait(3, a, s3st, sin)
        piece(quotient_of, a)
        big_back(3, 5, a, -1, lambda d: tags[d, pl.ds(0, 1), :], last_of(group - 1), g1, g2st, g2, g3st, cin)

    over(quotients)
    small_send(4, mst, m1)

    def values_of(a):
        dv = mm(sb_s[a], dn_s[a], 0, 0) + leave * mm(fk_s[a], cin[a], 1, 0)
        return [(dv_ref, a, dv.astype(BF16))]

    def keys_of(a):
        return [(gk_s, a, gk_s[a] + leave * mm(v_ref[a], cin[a], 1, 1))]

    def finish_of(a):
        k = k_ref[a].astype(F32)
        dfk = gk_s[a] + leave * cnm[pl.ds(a, 1), :]
        return [(dk_ref, a, (dfk * jnp.where(k > 0, 1.0, features(k))).astype(BF16))]

    small_wait(4, mst, m1)
    small_along(2, -1, m2st, m2, small_total(opening, m1), first_of(0))

    def values(a):
        back_wait(5, a, g3st, cin)
        piece(values_of, a)
        piece(keys_of, a)

    over(values)
    cnm[...] = small_total(later, m1) + small_along_take(2, -1, m2st, m2, same(last_of(group - 1), my_last), last_of(group - 1))
    staged(finish_of, heads, 4)

    each_to(1, lambda d: along(0, 0, d, 1, n2st, n2.at[d]).wait_send())
    each_to(-1, lambda d: along(2, 0, d, -1, m2st, m2.at[d]).wait_send())
    each_to(-1, lambda d: along(4, 0, d, -1, tagst, tags.at[d]).wait_send())

    def sent(a):
        each_to(1, lambda d: along(1, a, d, 1, s2st.at[a], s2.at[d, a]).wait_send())
        each_to(-1, lambda d: along(3, a, d, -1, g2st.at[a], g2.at[d, a]).wait_send())

    over(sent)


def local(queries, keys, values, out_grad, segment_ids):
    seqs, group = lax.axis_size("seq"), lax.axis_size("head")
    block = segment_ids.shape[0]
    rows, heads, dim = queries.shape
    longest = min(12 * block, block * seqs // 2)
    pair = PAIR
    while seqs % pair or heads % (group * pair):
        pair //= 2
    width, group, seqs = group, group * pair, seqs // pair
    own = heads // group
    window = min(-(-longest // (block * pair)), seqs - 1)
    turned = [x.transpose(1, 0, 2) for x in (queries, keys, values, out_grad)]
    vmem = pl.BlockSpec(memory_space=pltpu.VMEM)
    full = (heads, rows, dim)
    square = (heads, dim, dim)
    small = (heads, dim)
    tagged = (heads + 8, dim)
    piece = (own, dim, dim)
    state_scratch = [
        pltpu.VMEM(square, BF16), pltpu.VMEM((group,) + piece, BF16), pltpu.VMEM(piece, BF16),
        pltpu.VMEM((window + 1,) + piece, BF16), pltpu.VMEM((group,) + piece, BF16), pltpu.VMEM(square, BF16),
    ]
    def norm_scratch(first):
        return [
            pltpu.VMEM(first, F32), pltpu.VMEM((group,) + first, F32), pltpu.VMEM(tagged, F32),
            pltpu.VMEM((window + 1,) + tagged, F32), pltpu.VMEM(small, F32),
        ]

    outs = pl.pallas_call(
        functools.partial(kernel, seqs, pair, width, window),
        out_shape=[jax.ShapeDtypeStruct(full, BF16)] * 4,
        in_specs=[pl.BlockSpec(memory_space=pltpu.SMEM)] + [vmem] * 5,
        out_specs=[vmem] * 4,
        scratch_shapes=[
            pltpu.VMEM(full, BF16), pltpu.VMEM(full, BF16), pltpu.VMEM((heads, rows, rows), BF16),
            pltpu.VMEM(full, BF16), pltpu.VMEM((heads, rows, 1), F32), pltpu.VMEM(full, F32),
            pltpu.VMEM((heads, rows, rows), F32), pltpu.VMEM(full, F32),
        ] + norm_scratch(tagged) + norm_scratch(small) + state_scratch + state_scratch + [
            pltpu.VMEM((8, dim), F32), pltpu.VMEM((window + 1, 8, dim), F32),
            pltpu.SemaphoreType.DMA((6, own, group)), pltpu.SemaphoreType.DMA((6, own, group)),
            pltpu.SemaphoreType.DMA((5, own, window + 1)), pltpu.SemaphoreType.DMA((5, own, window + 1)),
        ],
        compiler_params=pltpu.CompilerParams(
            collective_id=0, has_side_effects=True, vmem_limit_bytes=48 * 1024 * 1024),
        name="segment_attention",
    )(segment_ids, segment_ids.reshape(width, rows).astype(F32), *turned)
    return tuple(x.transpose(1, 0, 2) for x in outs)


def solution(mesh):
    tokens = P(("seq", "head"), None, None)
    return jax.shard_map(
        local,
        mesh=mesh,
        in_specs=(tokens, tokens, tokens, tokens, P("seq")),
        out_specs=(tokens, tokens, tokens, tokens),
        check_vma=False,
    )
```

```python
import functools

import jax
import jax.numpy as jnp
from jax import lax
from jax.experimental import pallas as pl
from jax.experimental.pallas import tpu as pltpu
from jax.sharding import PartitionSpec as P

F32 = jnp.float32
BF16 = jnp.bfloat16
MESH = pl.DeviceIdType.MESH
PAIR = 2


def features(x):
    return jnp.where(x > 0, x + 1.0, jnp.exp(jnp.minimum(x, 0.0)))


def mm(a, b, ca, cb):
    return lax.dot_general(a, b, (((ca,), (cb,)), ((), ())), preferred_element_type=F32)


def kernel(seqs, pair, width, window, ids_ref, seg_ref, q_ref, k_ref, v_ref, g_ref,
           o_ref, dq_ref, dk_ref, dv_ref,
           fq_s, fk_s, sb_s, dn_s, inv_s, num_s, p2_s, gk_s,
           nst, n1, n2st, n2, nin,
           mst, m1, m2st, m2, cnm,
           sst, s1, s2st, s2, s3st, sin,
           gst, g1, g2st, g2, g3st, cin,
           tagst, tags,
           send1, recv1, send2, recv2):
    at_seq = lax.axis_index("seq")
    at_head = lax.axis_index("head")
    heads, rows, dim = q_ref.shape
    group = pair * width
    own = heads // group
    r = lax.div(at_seq, pair)
    h = lax.rem(at_seq, pair) * width + at_head

    def member(i):
        m = lax.rem(h + i, group)
        return (r * pair + lax.div(m, width), lax.rem(m, width))

    barrier = pltpu.get_barrier_semaphore()
    for i in range(1, group):
        pl.semaphore_signal(barrier, inc=1, device_id=member(i), device_id_type=MESH)
    for d in range(1, window + 1):
        @pl.when(r + d < seqs)
        def _():
            pl.semaphore_signal(barrier, inc=1, device_id=(at_seq + d * pair, at_head), device_id_type=MESH)

        @pl.when(r >= d)
        def _():
            pl.semaphore_signal(barrier, inc=1, device_id=(at_seq - d * pair, at_head), device_id_type=MESH)

    def same(x, y):
        return jnp.where(x == y, 1.0, 0.0)

    my_first = ids_ref[at_head * rows].astype(F32)
    my_last = ids_ref[at_head * rows + rows - 1].astype(F32)
    seg_r = seg_ref[pl.ds(at_head, 1), :]
    seg_c = jnp.transpose(jnp.broadcast_to(seg_r, (rows, rows)))[:, 0:1]
    enter = jnp.where(seg_c == my_first, 1.0, 0.0)
    leave = jnp.where(seg_c == my_last, 1.0, 0.0)
    keep = (lax.broadcasted_iota(jnp.int32, (rows, rows), 0)
            >= lax.broadcasted_iota(jnp.int32, (rows, rows), 1)) & (seg_c == seg_r)

    def inside(kind, a, i, src, dst):
        return pltpu.make_async_remote_copy(
            src_ref=src, dst_ref=dst, send_sem=send1.at[kind, a, i], recv_sem=recv1.at[kind, a, i],
            device_id=member(i), device_id_type=MESH)

    def along(kind, a, d, sign, src, dst):
        return pltpu.make_async_remote_copy(
            src_ref=src, dst_ref=dst, send_sem=send2.at[kind, a, d], recv_sem=recv2.at[kind, a, d],
            device_id=(at_seq + sign * d * pair, at_head), device_id_type=MESH)

    def has_to(d, sign):
        return (r + d < seqs) if sign > 0 else (r >= d)

    def has_from(d, sign):
        return (r >= d) if sign > 0 else (r + d < seqs)

    def each_to(sign, act):
        for d in range(1, window + 1):
            pl.when(has_to(d, sign))(functools.partial(act, d))

    def each_from(sign, act):
        for d in range(1, window + 1):
            pl.when(has_from(d, sign))(functools.partial(act, d))

    for d in range(1, window + 1):
        @pl.when(r < d)
        def _():
            n2[d] = jnp.full(n2.shape[1:], -1.0, F32)

        @pl.when(r + d >= seqs)
        def _():
            m2[d] = jnp.full(m2.shape[1:], -1.0, F32)
            tags[d] = jnp.full(tags.shape[1:], -1.0, F32)

    def staged(work, count, step):
        def body(t, c):
            done = [work(t * step + u) for u in range(step)]
            for puts in done:
                for ref, at, value in puts:
                    ref[at] = value
            return c

        lax.fori_loop(0, count // step, body, 0)

    def piece(work, a):
        for low in range(0, group, 4):
            done = [work(j * own + a) for j in range(low, min(low + 4, group))]
            for puts in done:
                for ref, at, value in puts:
                    ref[at] = value

    def row_of(a):
        return (pl.ds(a, 1), slice(None))

    def first_of(j):
        return n1[j, pl.ds(heads, 1), :]

    def last_of(j):
        return n1[j, pl.ds(heads + 1, 1), :]

    def small_total(weigh, buf):
        total = weigh(0) * buf[0, pl.ds(0, heads), :]
        for j in range(1, group):
            total = total + weigh(j) * buf[j, pl.ds(0, heads), :]
        return total

    def closing(j):
        return same(last_of(j), last_of(group - 1))

    def opening(j):
        return same(first_of(j), first_of(0))

    def earlier(j):
        return jnp.where(j < h, 1.0, 0.0) * same(last_of(j), my_first)

    def later(j):
        return jnp.where(j > h, 1.0, 0.0) * same(first_of(j), my_last)

    def small_send(kind, st, buf):
        for i in range(1, group):
            inside(kind, 0, i, st, buf.at[h]).start()
        buf[h] = st[...]

    def small_wait(kind, st, buf):
        for i in range(1, group):
            inside(kind, 0, i, st, buf.at[0]).wait()

    def small_along(kind, sign, st, buf, value, tag):
        st[pl.ds(0, heads), :] = value
        st[pl.ds(heads, 8), :] = jnp.broadcast_to(tag, (8, dim))
        each_to(sign, lambda d: along(kind, 0, d, sign, st, buf.at[d]).start())

    def small_along_take(kind, sign, st, buf, scale, own_tag):
        each_from(sign, lambda d: along(kind, 0, d, sign, st, buf.at[d]).wait_recv())
        total = jnp.zeros((heads, dim), F32)
        for d in range(1, window + 1):
            linked = buf[d, pl.ds(heads, 1), :] == own_tag
            total = total + jnp.where(linked, buf[d, pl.ds(0, heads), :], 0.0)
        return total * scale

    def big_send(kind, a, st, buf):
        for i in range(1, group):
            inside(kind, a, i, st.at[lax.rem(h + i, group) * own + a], buf.at[h, a]).start()

    def big_along(kind, kind1, a, sign, weigh, st, mid, out, buf):
        for i in range(1, group):
            inside(kind1, a, i, st.at[a], mid.at[0, a]).wait()
        mid[h, a] = st[h * own + a]
        total = weigh(0) * mid[0, a].astype(F32)
        for j in range(1, group):
            total = total + weigh(j) * mid[j, a].astype(F32)
        out[a] = total.astype(BF16)
        each_to(sign, lambda d: along(kind, a, d, sign, out.at[a], buf.at[d, a]).start())

    def big_back(kind, kind1, a, sign, tag_of, tag, mid, out, buf, st3, fin):
        each_from(sign, lambda d: along(kind, a, d, sign, out.at[a], buf.at[d, a]).wait_recv())
        far = jnp.zeros((dim, dim), F32)
        for d in range(1, window + 1):
            far = far + jnp.where(tag_of(d) == tag, buf[d, a].astype(F32), 0.0)
        near = [mid[m, a].astype(F32) for m in range(group)]
        for j in range(group):
            if sign > 0:
                total = opening(j) * far
                for m in range(j):
                    total = total + same(last_of(m), first_of(j)) * near[m]
            else:
                total = closing(j) * far
                for m in range(j + 1, group):
                    total = total + same(first_of(m), last_of(j)) * near[m]
            st3[j, a] = total.astype(BF16)
        for i in range(1, group):
            inside(kind1, a, i, st3.at[lax.rem(h + i, group), a], fin.at[h * own + a]).start()
        fin[h * own + a] = st3[h, a]

    def back_wait(kind1, a, st3, fin):
        for i in range(1, group):
            inside(kind1, a, i, st3.at[0, a], fin.at[a]).wait()

    def over(body):
        def turn(a, c):
            body(a)
            return c

        lax.fori_loop(0, own, turn, 0)

    def features_of(a):
        fk = features(k_ref[a].astype(F32))
        fq = features(q_ref[a].astype(F32))
        return [(fq_s, a, fq.astype(BF16)), (fk_s, a, fk.astype(BF16)),
                (nst, row_of(a), jnp.sum(fk * leave, axis=0, keepdims=True))]

    def state_of(a):
        ending = (fk_s[a].astype(F32) * leave).astype(BF16)
        return [(sst, a, mm(ending, v_ref[a], 0, 0).astype(BF16))]

    staged(features_of, heads, 4)

    peers = group - 1
    for d in range(1, window + 1):
        peers = peers + jnp.where(r >= d, 1, 0) + jnp.where(r + d < seqs, 1, 0)
    pl.semaphore_wait(barrier, peers)

    nst[pl.ds(heads, 1), :] = jnp.full((1, dim), my_first, F32)
    nst[pl.ds(heads + 1, 1), :] = jnp.full((1, dim), my_last, F32)
    small_send(0, nst, n1)

    def open_states(a):
        piece(state_of, a)
        big_send(1, a, sst, s1)

    over(open_states)

    def scores_of(a):
        s = jnp.where(keep, mm(fq_s[a], fk_s[a], 1, 1), 0.0)
        return [(inv_s, a, jnp.sum(s, axis=1, keepdims=True)), (sb_s, a, s.astype(BF16))]

    small_wait(0, nst, n1)
    small_along(0, 1, n2st, n2, small_total(closing, n1), last_of(group - 1))
    tagst[...] = jnp.broadcast_to(first_of(0), tagst.shape)
    each_to(-1, lambda d: along(4, 0, d, -1, tagst, tags.at[d]).start())
    staged(scores_of, heads, 4)
    nin[...] = small_total(earlier, n1) + small_along_take(0, 1, n2st, n2, same(first_of(0), my_first), first_of(0))

    def gradient_state_of(a):
        fq = features(q_ref[a].astype(F32)) * enter
        denom = inv_s[a] + jnp.sum(fq * nin[pl.ds(a, 1), :], axis=1, keepdims=True)
        inv = 1.0 / denom
        dn = (g_ref[a].astype(F32) * inv).astype(BF16)
        return [(inv_s, a, inv), (dn_s, a, dn), (gst, a, mm(fq.astype(BF16), dn, 0, 0).astype(BF16))]

    def gradient_states(a):
        piece(gradient_state_of, a)
        big_send(2, a, gst, g1)
        big_along(1, 1, a, 1, closing, sst, s1, s2st, s2)

    over(gradient_states)

    def inner_of(a):
        return [(num_s, a, mm(sb_s[a], v_ref[a], 1, 0)), (p2_s, a, mm(dn_s[a], v_ref[a], 1, 1))]

    staged(inner_of, heads, 4)
    over(lambda a: big_along(3, 2, a, -1, opening, gst, g1, g2st, g2))

    over(lambda a: big_back(1, 3, a, 1, lambda d: n2[d, pl.ds(heads, 1), :], first_of(0), s1, s2st, s2, s3st, sin))
    each_from(-1, lambda d: along(4, 0, d, -1, tagst, tags.at[d]).wait_recv())

    def quotient_of(a):
        q = q_ref[a].astype(F32)
        fq = features(q)
        st = sin[a]
        inv = inv_s[a]
        numer = num_s[a] + enter * mm(fq_s[a], st, 1, 0)
        quo = numer * inv
        dden = -jnp.sum(g_ref[a].astype(F32) * quo, axis=1, keepdims=True) * inv
        inner = enter * dden
        ds = jnp.where(keep, p2_s[a] + dden, 0.0).astype(BF16)
        dfq = mm(ds, fk_s[a], 1, 0) + enter * mm(dn_s[a], st, 1, 1) + inner * nin[pl.ds(a, 1), :]
        return [(o_ref, a, quo.astype(BF16)),
                (mst, row_of(a), jnp.sum(fq * inner, axis=0, keepdims=True)),
                (dq_ref, a, (dfq * jnp.where(q > 0, 1.0, fq)).astype(BF16)),
                (gk_s, a, mm(ds, fq_s[a], 0, 0))]

    def quotients(a):
        back_wait(3, a, s3st, sin)
        piece(quotient_of, a)

    over(lambda a: big_back(3, 5, a, -1, lambda d: tags[d, pl.ds(0, 1), :], last_of(group - 1), g1, g2st, g2, g3st, cin))
    over(quotients)
    small_send(4, mst, m1)

    def values_of(a):
        dv = mm(sb_s[a], dn_s[a], 0, 0) + leave * mm(fk_s[a], cin[a], 1, 0)
        return [(dv_ref, a, dv.astype(BF16))]

    def keys_of(a):
        return [(gk_s, a, gk_s[a] + leave * mm(v_ref[a], cin[a], 1, 1))]

    def finish_of(a):
        k = k_ref[a].astype(F32)
        dfk = gk_s[a] + leave * cnm[pl.ds(a, 1), :]
        return [(dk_ref, a, (dfk * jnp.where(k > 0, 1.0, features(k))).astype(BF16))]

    def values(a):
        back_wait(5, a, g3st, cin)
        piece(values_of, a)
        piece(keys_of, a)

    values(0)
    small_wait(4, mst, m1)
    small_along(2, -1, m2st, m2, small_total(opening, m1), first_of(0))
    lax.fori_loop(1, own, lambda a, c: (values(a), c)[1], 0)
    cnm[...] = small_total(later, m1) + small_along_take(2, -1, m2st, m2, same(last_of(group - 1), my_last), last_of(group - 1))
    staged(finish_of, heads, 4)

    each_to(1, lambda d: along(0, 0, d, 1, n2st, n2.at[d]).wait_send())
    each_to(-1, lambda d: along(2, 0, d, -1, m2st, m2.at[d]).wait_send())
    each_to(-1, lambda d: along(4, 0, d, -1, tagst, tags.at[d]).wait_send())

    def sent(a):
        each_to(1, lambda d: along(1, a, d, 1, s2st.at[a], s2.at[d, a]).wait_send())
        each_to(-1, lambda d: along(3, a, d, -1, g2st.at[a], g2.at[d, a]).wait_send())

    over(sent)


def local(queries, keys, values, out_grad, segment_ids):
    seqs, group = lax.axis_size("seq"), lax.axis_size("head")
    block = segment_ids.shape[0]
    rows, heads, dim = queries.shape
    longest = min(12 * block, block * seqs // 2)
    pair = PAIR
    while seqs % pair or heads % (group * pair):
        pair //= 2
    width, group, seqs = group, group * pair, seqs // pair
    own = heads // group
    window = min(-(-longest // (block * pair)), seqs - 1)
    turned = [x.transpose(1, 0, 2) for x in (queries, keys, values, out_grad)]
    vmem = pl.BlockSpec(memory_space=pltpu.VMEM)
    full = (heads, rows, dim)
    square = (heads, dim, dim)
    small = (heads, dim)
    tagged = (heads + 8, dim)
    piece = (own, dim, dim)
    state_scratch = [
        pltpu.VMEM(square, BF16), pltpu.VMEM((group,) + piece, BF16), pltpu.VMEM(piece, BF16),
        pltpu.VMEM((window + 1,) + piece, BF16), pltpu.VMEM((group,) + piece, BF16), pltpu.VMEM(square, BF16),
    ]
    def norm_scratch(first):
        return [
            pltpu.VMEM(first, F32), pltpu.VMEM((group,) + first, F32), pltpu.VMEM(tagged, F32),
            pltpu.VMEM((window + 1,) + tagged, F32), pltpu.VMEM(small, F32),
        ]

    outs = pl.pallas_call(
        functools.partial(kernel, seqs, pair, width, window),
        out_shape=[jax.ShapeDtypeStruct(full, BF16)] * 4,
        in_specs=[pl.BlockSpec(memory_space=pltpu.SMEM)] + [vmem] * 5,
        out_specs=[vmem] * 4,
        scratch_shapes=[
            pltpu.VMEM(full, BF16), pltpu.VMEM(full, BF16), pltpu.VMEM((heads, rows, rows), BF16),
            pltpu.VMEM(full, BF16), pltpu.VMEM((heads, rows, 1), F32), pltpu.VMEM(full, F32),
            pltpu.VMEM((heads, rows, rows), F32), pltpu.VMEM(full, F32),
        ] + norm_scratch(tagged) + norm_scratch(small) + state_scratch + state_scratch + [
            pltpu.VMEM((8, dim), F32), pltpu.VMEM((window + 1, 8, dim), F32),
            pltpu.SemaphoreType.DMA((6, own, group)), pltpu.SemaphoreType.DMA((6, own, group)),
            pltpu.SemaphoreType.DMA((5, own, window + 1)), pltpu.SemaphoreType.DMA((5, own, window + 1)),
        ],
        compiler_params=pltpu.CompilerParams(
            collective_id=0, has_side_effects=True, vmem_limit_bytes=48 * 1024 * 1024),
        name="segment_attention",
    )(segment_ids, segment_ids.reshape(width, rows).astype(F32), *turned)
    return tuple(x.transpose(1, 0, 2) for x in outs)


def solution(mesh):
    tokens = P(("seq", "head"), None, None)
    return jax.shard_map(
        local,
        mesh=mesh,
        in_specs=(tokens, tokens, tokens, tokens, P("seq")),
        out_specs=(tokens, tokens, tokens, tokens),
        check_vma=False,
    )
```
